128 devices in a mesh: expert: 16 (over z, y), pipe: 8 (over x, core).
Axes of the slice: x: 4, y: 4, z: 4, core: 2. Of those that a mesh axis runs over, the one named last changes fastest.
Arguments:
- layer_input: bfloat16 [8, 4096, 7168], P('pipe', 'expert'), may hold values from -6 to 6
- output_grad: bfloat16 [8, 4096, 7168], P('pipe', 'expert'), may hold values from -6 to 6
- gate_weight: bfloat16 [8, 7168, 2048], P('pipe', None, 'expert'), may hold values from -0.0625 to 0.0625
- up_weight: bfloat16 [8, 7168, 2048], P('pipe', None, 'expert'), may hold values from -0.0625 to 0.0625
- down_weight: bfloat16 [8, 2048, 7168], P('pipe', 'expert'), may hold values from -0.1875 to 0.1875
- expert_ids: int32 [8, 4096, 8], P('pipe', 'expert'), may hold values from 0 to 255, as said below
- slots: int32 [8, 4096, 8], P('pipe', 'expert'), may hold values from 0 to 32, as said below
- combine_weights: bfloat16 [8, 4096, 8], P('pipe', 'expert'), may hold values from 0.099609375 to 0.59765625
Outputs:
- prev_grad: bfloat16 [8, 4096, 7168], P('pipe', 'expert')
- gate_grad: bfloat16 [8, 7168, 2048], P('pipe', None, 'expert')
- up_grad: bfloat16 [8, 7168, 2048], P('pipe', None, 'expert')
- down_grad: bfloat16 [8, 2048, 7168], P('pipe', 'expert')
- router_grad: float32 [8, 4096, 8], P('pipe', 'expert')
The draws below stay inside these ranges and needn't reach their ends.
Inputs may be any that keep to these rules, and one draw needn't show every extreme that they name: `expert_ids`: each token names 8 different experts. In every section one expert below 2 is named by more than 32 tokens of every device's 256 tokens. `slots`: A token's slot for an expert counts the earlier tokens of the same device's 256 tokens that name that expert, capped at 32, which marks a dropped token.
All inputs are finite; a program needn't handle non-finite values.
Results may differ from the reference program's by a relative error of at most 0.015.
Values may be sent and summed in bfloat16 or wider, within the bound.
No kernel may reach another device: no remote copies, remote signals or barrier semaphores. Data moves between devices by JAX's collectives and lax.ppermute only.
A program may use at most 128 MiB of HBM per device.

```python
import jax
import jax.numpy as jnp
from jax import lax

D = 7168
FF = 1024
EXPERTS = 256
TOPK = 8
GROUP = 8
TOK_DEV = 256
CAP = 32
EXP_WIN = 2
HIDDEN_SIZE = 2048
TOKENS = 4096
SECTIONS = 8
N_EXPERT = 16


def routing_tables(key):
    noise = jax.random.randint(jax.random.fold_in(key, 101), (SECTIONS, TOKENS, EXPERTS), 0, 2 ** 20)
    scores = noise * EXPERTS + jnp.arange(EXPERTS, dtype=jnp.int32)
    favourite = jax.random.randint(jax.random.fold_in(key, 102), (SECTIONS, 1, 1), 0, EXP_WIN)
    blocks = TOKENS // TOK_DEV
    order_noise = jax.random.randint(jax.random.fold_in(key, 103), (SECTIONS, blocks, TOK_DEV), 0, 2 ** 16)
    distinct = order_noise * TOK_DEV + jnp.arange(TOK_DEV, dtype=jnp.int32)
    ranking = jnp.argsort(jnp.argsort(distinct, axis=-1), axis=-1).astype(jnp.int32).reshape(SECTIONS, TOKENS, 1)
    chosen = (ranking < CAP + CAP // 2) & (jnp.arange(EXPERTS, dtype=jnp.int32)[None, None, :] == favourite)
    scores = scores + chosen.astype(jnp.int32) * 2 ** 29
    picked = lax.top_k(scores, TOPK)[1].astype(jnp.int32)
    counting = jnp.zeros((SECTIONS, TOKENS, EXPERTS), jnp.int32)
    for column in range(TOPK):
        counting = counting + (picked[:, :, column:column + 1] == jnp.arange(EXPERTS, dtype=jnp.int32)[None, None, :]).astype(jnp.int32)
    counting = counting.reshape(SECTIONS, blocks, TOK_DEV, EXPERTS)
    earlier = (jnp.cumsum(counting, axis=2) - counting).reshape(SECTIONS, TOKENS, EXPERTS)
    placed = jnp.take_along_axis(earlier, picked, axis=2)
    return (picked, jnp.minimum(placed, CAP).astype(jnp.int32))


def draw_expert_ids(key, part):
    return routing_tables(key)[0]


def draw_slots(key, part):
    return routing_tables(key)[1]


def block_scale(rng, dims, pieces, least, high):
    gain = 1.0
    for axis_at, parts in pieces:
        heights = jax.random.uniform(jax.random.fold_in(jax.random.fold_in(rng, 6), axis_at), (parts,), jnp.float32, least / len(pieces), high / len(pieces))
        gain = gain * jnp.repeat(jnp.exp(heights), dims[axis_at] // parts).reshape((-1,) + (1,) * (len(dims) - 1 - axis_at))
    return gain


def gaussian(own_key, extent, width, most, cuts=(), kind=jnp.bfloat16):
    array = jax.random.normal(own_key, extent, jnp.float32) * width
    if len(cuts) > 0:
        array = block_scale(own_key, extent, cuts, -0.22, 0.18) * array
    return jnp.clip(array, min=-most, max=most).astype(kind)


def setup_inputs(seed: int = 0) -> dict:
    streams_of = jax.random.split(jax.random.key(seed), 9)
    layer_input = gaussian(streams_of[0], (SECTIONS, TOKENS, D), 1.0, 6.0, ((0, 8), (1, 16)))
    output_grad = gaussian(streams_of[1], (SECTIONS, TOKENS, D), 1.0, 6.0, ((0, 8), (1, 16)))
    gate_weight = gaussian(streams_of[2], (SECTIONS, D, HIDDEN_SIZE), D ** -0.5, 0.0625, ((0, 8), (2, 16)))
    up_weight = gaussian(streams_of[3], (SECTIONS, D, HIDDEN_SIZE), D ** -0.5, 0.0625, ((0, 8), (2, 16)))
    down_weight = gaussian(streams_of[4], (SECTIONS, HIDDEN_SIZE, D), FF ** -0.5, 0.1875, ((0, 8), (1, 16)))
    expert_ids = draw_expert_ids(jax.random.fold_in(streams_of[8], 71), 0)
    slots = draw_slots(jax.random.fold_in(streams_of[8], 71), 0)
    combine_weights = jnp.clip(0.099609375 + 0.49804688 * jax.random.uniform(streams_of[7], (SECTIONS, TOKENS, TOPK), jnp.float32) ** block_scale(streams_of[7], (SECTIONS, TOKENS, TOPK), ((0, 8), (1, 16)), -0.2, 0.2), 0.099609375, 0.59765625).astype(jnp.bfloat16)
    return {"layer_input": layer_input, "output_grad": output_grad, "gate_weight": gate_weight, "up_weight": up_weight, "down_weight": down_weight, "expert_ids": expert_ids, "slots": slots, "combine_weights": combine_weights}


def rounded(value):
    return lax.optimization_barrier(value.astype(jnp.bfloat16)).astype(jnp.float32)


def section_backward(inputs, upstream, w_gate, w_up, w_down, routes, places, weights):
    blocks = jnp.arange(TOKENS, dtype=jnp.int32) // TOK_DEV
    rows_total = N_EXPERT * CAP
    member = FF // GROUP
    contribution = jnp.zeros((TOKENS, D), jnp.float32)
    router_grad = jnp.zeros((TOKENS, TOPK), jnp.float32)
    gate_list, up_list, down_list = [], [], []
    for expert in range(EXP_WIN):
        token_buffer = jnp.zeros((rows_total, D), jnp.bfloat16)
        grad_buffer = jnp.zeros((rows_total, D), jnp.bfloat16)
        weight_buffer = jnp.zeros((rows_total,), jnp.bfloat16)
        targets = []
        for column in range(TOPK):
            hit = (routes[:, column] == expert) & (places[:, column] < CAP)
            target = jnp.where(hit, blocks * CAP + places[:, column], rows_total).astype(jnp.int32)
            token_buffer = token_buffer.at[target].set(inputs, mode="drop")
            grad_buffer = grad_buffer.at[target].set(upstream, mode="drop")
            weight_buffer = weight_buffer.at[target].set(weights[:, column], mode="drop")
            targets.append((hit, target))
        lower = expert * FF
        gate_cols = w_gate[:, lower:lower + FF]
        up_cols = w_up[:, lower:lower + FF]
        down_rows = w_down[lower:lower + FF, :]
        gate_pre = jnp.dot(token_buffer, gate_cols, preferred_element_type=jnp.float32)
        up_pre = jnp.dot(token_buffer, up_cols, preferred_element_type=jnp.float32)
        sigmoid_gate = jax.nn.sigmoid(gate_pre)
        silu_gate = gate_pre * sigmoid_gate
        hidden = (silu_gate * up_pre).astype(jnp.bfloat16)
        scaled = (weight_buffer.astype(jnp.float32)[:, None] * grad_buffer.astype(jnp.float32)).astype(jnp.bfloat16)
        hidden_split = hidden.astype(jnp.float32).reshape(rows_total, GROUP, member)
        down_split = down_rows.astype(jnp.float32).reshape(GROUP, member, D)
        partial_out = jnp.einsum("rgf,gfd->grd", hidden_split, down_split)
        score_parts = jnp.sum(partial_out * grad_buffer.astype(jnp.float32)[None], axis=2)
        score_sum = jnp.sum(rounded(score_parts), axis=0)
        back_hidden = jnp.dot(scaled, down_rows.T, preferred_element_type=jnp.float32)
        dgate = (back_hidden * up_pre * sigmoid_gate * (1.0 + gate_pre * (1.0 - sigmoid_gate))).astype(jnp.bfloat16)
        dup = (back_hidden * silu_gate).astype(jnp.bfloat16)
        down_list.append(jnp.dot(hidden.T, scaled, preferred_element_type=jnp.float32).astype(jnp.bfloat16))
        gate_list.append(jnp.dot(token_buffer.T, dgate, preferred_element_type=jnp.float32).astype(jnp.bfloat16))
        up_list.append(jnp.dot(token_buffer.T, dup, preferred_element_type=jnp.float32).astype(jnp.bfloat16))
        back_parts = jnp.einsum("rgf,dgf->grd", dgate.astype(jnp.float32).reshape(rows_total, GROUP, member), gate_cols.astype(jnp.float32).reshape(D, GROUP, member))
        back_parts = back_parts + jnp.einsum("rgf,dgf->grd", dup.astype(jnp.float32).reshape(rows_total, GROUP, member), up_cols.astype(jnp.float32).reshape(D, GROUP, member))
        back_sum = jnp.sum(rounded(back_parts), axis=0)
        for column in range(TOPK):
            hit, target = targets[column]
            safe = jnp.minimum(target, rows_total - 1).astype(jnp.int32)
            contribution = contribution + jnp.where(hit[:, None], back_sum[safe], 0.0)
            router_grad = router_grad.at[:, column].add(jnp.where(hit, score_sum[safe], 0.0))
    input_grad = (upstream.astype(jnp.float32) + contribution).astype(jnp.bfloat16)
    gate_grad = jnp.concatenate(gate_list, axis=1)
    up_grad = jnp.concatenate(up_list, axis=1)
    down_grad = jnp.concatenate(down_list, axis=0)
    return input_grad, gate_grad, up_grad, down_grad, router_grad


def reference(layer_input, output_grad, gate_weight, up_weight, down_weight, expert_ids, slots, combine_weights):
    inputs_list, gate_list, up_list, down_list, router_list = [], [], [], [], []
    for section in range(SECTIONS):
        results = section_backward(layer_input[section], output_grad[section], gate_weight[section], up_weight[section], down_weight[section], expert_ids[section], slots[section], combine_weights[section])
        inputs_list.append(results[0])
        gate_list.append(results[1])
        up_list.append(results[2])
        down_list.append(results[3])
        router_list.append(results[4])
    shifted = inputs_list[1:] + [jnp.zeros((TOKENS, D), jnp.bfloat16)]
    return (jnp.stack(shifted), jnp.stack(gate_list), jnp.stack(up_list), jnp.stack(down_list), jnp.stack(router_list))
```

```python
import functools

import jax
import jax.numpy as jnp
from jax import lax
from jax.experimental import pallas as pl
from jax.experimental.pallas import tpu as pltpu
from jax.sharding import PartitionSpec as P


CAP = 32
SIDE = 4
BF = jnp.bfloat16
F32 = jnp.float32

FAR, RIGHT, LEFT, HERE = range(4)
OWN, MIRROR, PAIR, PAIRMIRROR = range(4)


def ring(step):
    return [(z * SIDE + y, z * SIDE + (y + step) % SIDE) for z in range(SIDE) for y in range(SIDE)]


RIGHTWARD, LEFTWARD, ACROSS = ring(1), ring(-1), ring(2)
PAIRED = [(e, e ^ SIDE) for e in range(SIDE * SIDE)]
MIRRORED = [(z * SIDE + y, (SIDE - 1 - z) * SIDE + y) for z in range(SIDE) for y in range(SIDE)]


def move(x, pairs):
    return lax.ppermute(x, "expert", pairs)


def back_one(x):
    size = lax.axis_size("pipe")
    return lax.ppermute(x, "pipe", [(i, i - 1) for i in range(1, size)])


def back_one_mirrored(x):
    size = lax.axis_size("pipe")
    pairs = [(e * size + i, m * size + i - 1) for e, m in MIRRORED for i in range(1, size)]
    return lax.ppermute(x, ("expert", "pipe"), pairs)


def matches(position, own, rows):
    column = lax.broadcasted_iota(jnp.int32, (rows, 2 * CAP), 1)
    expert = jnp.where(column < CAP, own, 1 - own)
    wanted = expert * CAP + column % CAP
    return [position[:, k : k + 1] == wanted for k in range(position.shape[1])]


def pick_kernel(own_ref, pos_ref, w_ref, x_ref, g_ref, oy, cy, oz, cz, hot, scale, *, steps):
    j = pl.program_id(0)

    @pl.when(j == 0)
    def _():
        rows = pos_ref.shape[0]
        weights = w_ref[...].astype(F32)
        one = jnp.zeros((rows, 2 * CAP), F32)
        weight = jnp.zeros((rows, 2 * CAP), F32)
        for k, hit in enumerate(matches(pos_ref[...], own_ref[0], rows)):
            one = one + jnp.where(hit, 1.0, 0.0)
            weight = weight + jnp.where(hit, weights[:, k : k + 1], 0.0)
        hot[...] = one.astype(BF)
        scale[...] = lax.dot_general(
            weight.astype(BF),
            jnp.ones((rows, 128), BF),
            (((0,), (0,)), ((), ())),
            preferred_element_type=F32,
        )

    dims = (((0,), (0,)), ((), ()))
    x = lax.dot_general(hot[...], x_ref[...], dims, preferred_element_type=F32).astype(BF)
    g = lax.dot_general(hot[...], g_ref[...], dims, preferred_element_type=F32)
    s = (g * scale[:, 0:1]).astype(BF)

    def put(o, c):
        o[0:CAP, :] = x[0:CAP]
        o[CAP : 2 * CAP, :] = s[0:CAP]
        c[0:CAP, :] = x[CAP : 2 * CAP]
        c[CAP : 2 * CAP, :] = s[CAP : 2 * CAP]

    @pl.when(j < steps)
    def _():
        put(oy, cy)

    @pl.when(j >= steps)
    def _():
        put(oz, cz)


def pick(own, position, weights, x, g, split, block=1024):
    tokens, width = x.shape
    steps, total = split // block, width // block
    whole = lambda a: pl.BlockSpec(a.shape, lambda j, *_: (0, 0))
    near = pl.BlockSpec((2 * CAP, block), lambda j, *_: (0, jnp.minimum(j, steps - 1)))
    late = pl.BlockSpec((2 * CAP, block), lambda j, *_: (0, jnp.maximum(j - steps, 0)))
    cols = pl.BlockSpec((tokens, block), lambda j, *_: (0, j))
    shape = lambda n: jax.ShapeDtypeStruct((2 * CAP, n), BF)
    return pl.pallas_call(
        functools.partial(pick_kernel, steps=steps),
        grid_spec=pltpu.PrefetchScalarGridSpec(
            num_scalar_prefetch=1,
            grid=(total,),
            in_specs=[whole(position), whole(weights), cols, cols],
            out_specs=[near, near, late, late],
            scratch_shapes=[pltpu.VMEM((tokens, 2 * CAP), BF), pltpu.VMEM((2 * CAP, 128), F32)],
        ),
        out_shape=[shape(split), shape(split), shape(width - split), shape(width - split)],
        name="pick",
    )(own, position, weights, x, g)


def spread(piece):
    left = move(piece, RIGHTWARD)
    right = move(piece, LEFTWARD)
    far_x = move(left[:CAP], RIGHTWARD)
    far_s = move(right[CAP:], LEFTWARD)
    return {HERE: piece, LEFT: left, RIGHT: right, FAR: (far_x, far_s)}


def forward_kernel(*refs, places, split, chunk):
    n = len(places)
    pieces, (wg, wu, wd) = refs[:n], refs[n : n + 3]
    xo, so, dgu, hid, score = refs[n + 3 : n + 8]
    x, s, wgu, wdv, agu, ab, sems, osem = refs[n + 8 :]
    width = x.shape[1]

    def weight_copies(k, lo, hi):
        at = pl.ds(lo, hi - lo)
        return [
            pltpu.make_async_copy(wg.at[at], wgu.at[at, 0:128], sems.at[k]),
            pltpu.make_async_copy(wu.at[at], wgu.at[at, 128:256], sems.at[k + 1]),
            pltpu.make_async_copy(wd.at[:, at], wdv.at[:, at], sems.at[k + 2]),
        ]

    early = weight_copies(0, split, width)
    late = weight_copies(3, 0, split)
    k = 6
    for ref, (row, lo, hi, kind) in zip(pieces, places):
        here = early if lo == split else late
        parts = {"xs": ((x, 0), (s, CAP)), "x": ((x, 0),), "s": ((s, 0),)}[kind]
        for dst, at in parts:
            here.append(
                pltpu.make_async_copy(
                    ref.at[at : at + CAP], dst.at[row : row + CAP, lo:hi], sems.at[k]
                )
            )
            k += 1
    for copy in early + late:
        copy.start()
    agu[...] = jnp.zeros_like(agu)
    ab[...] = jnp.zeros_like(ab)

    def multiply(lo, hi):
        def body(i, _):
            at = pl.ds(pl.multiple_of(lo + i * chunk, chunk), chunk)
            agu[...] += jnp.dot(x[:, at], wgu[at, :], preferred_element_type=F32)
            ab[...] += lax.dot_general(
                s[:, at], wdv[:, at], (((1,), (1,)), ((), ())), preferred_element_type=F32
            )
            return 0

        lax.fori_loop(0, (hi - lo) // chunk, body, 0)

    outs = []
    for copies, lo, hi, k in ((early, split, width, 0), (late, 0, split, 2)):
        for copy in copies:
            copy.wait()
        for a, (src, dst) in enumerate(((x, xo), (s, so))):
            out = pltpu.make_async_copy(src.at[:, lo:hi], dst.at[:, lo:hi], osem.at[k + a])
            out.start()
            outs.append(out)
        multiply(lo, hi)
    gate, up, back = agu[:, 0:128], agu[:, 128:256], ab[...]
    sigmoid = jax.nn.sigmoid(gate)
    silu = gate * sigmoid
    hidden = (silu * up).astype(BF)
    hid[...] = hidden
    dgu[:, 0:128] = (back * up * sigmoid * (1.0 + gate * (1.0 - sigmoid))).astype(BF)
    dgu[:, 128:256] = (back * silu).astype(BF)
    total = jnp.sum(hidden.astype(F32) * back, axis=1, keepdims=True)
    score[...] = jnp.broadcast_to(total, score.shape)
    for out in outs:
        out.wait()


def forward(pieces, places, wg, wu, wd, split, chunk=512):
    width, units = wg.shape
    rows = 16 * CAP
    copies = 6 + sum(len(kind) for *_, kind in places)
    anywhere = pl.BlockSpec(memory_space=pl.ANY)
    vmem = pl.BlockSpec(memory_space=pltpu.VMEM)
    return pl.pallas_call(
        functools.partial(forward_kernel, places=places, split=split, chunk=chunk),
        in_specs=[anywhere] * (len(pieces) + 3),
        out_specs=[anywhere, anywhere, vmem, vmem, vmem],
        out_shape=[
            jax.ShapeDtypeStruct((rows, width), BF),
            jax.ShapeDtypeStruct((rows, width), BF),
            jax.ShapeDtypeStruct((rows, 2 * units), BF),
            jax.ShapeDtypeStruct((rows, units), BF),
            jax.ShapeDtypeStruct((rows, 128), F32),
        ],
        scratch_shapes=[
            pltpu.VMEM((rows, width), BF),
            pltpu.VMEM((rows, width), BF),
            pltpu.VMEM((width, 2 * units), BF),
            pltpu.VMEM((units, width), BF),
            pltpu.VMEM((rows, 2 * units), F32),
            pltpu.VMEM((rows, units), F32),
            pltpu.SemaphoreType.DMA((copies,)),
            pltpu.SemaphoreType.DMA((4,)),
        ],
        name="forward",
    )(*pieces, wg, wu, wd)


def return_kernel(dgu, wg, wu, *outs):
    dims = (((1,), (1,)), ((), ()))
    value = lax.dot_general(dgu[:, 0:128], wg[...], dims, preferred_element_type=F32)
    value += lax.dot_general(dgu[:, 128:256], wu[...], dims, preferred_element_type=F32)
    value = value.astype(BF)
    for i, out in enumerate(outs):
        out[...] = value[i * 2 * CAP : (i + 1) * 2 * CAP]


def give_back(dgu, wg, wu, lo, hi, block, name):
    rows, units = dgu.shape[0], wg.shape[1]
    first = lo // block
    weight = pl.BlockSpec((block, units), lambda j: (first + j, 0))
    return pl.pallas_call(
        return_kernel,
        grid=((hi - lo) // block,),
        in_specs=[pl.BlockSpec(dgu.shape, lambda j: (0, 0)), weight, weight],
        out_specs=[pl.BlockSpec((2 * CAP, block), lambda j: (0, j))] * 8,
        out_shape=[jax.ShapeDtypeStruct((2 * CAP, hi - lo), BF)] * 8,
        name=name,
    )(dgu, wg, wu)


def add(*terms):
    total = terms[0].astype(F32)
    for term in terms[1:]:
        total = total + term.astype(F32)
    return total.astype(BF)


def shards(x, g, wg, wu, wd, expert_ids, slots, combine):
    x, g, wg, wu, wd = x[0], g[0], wg[0], wu[0], wd[0]
    ids, places, weights = expert_ids[0], slots[0], combine[0]
    tokens, width = x.shape
    split = width // 7 * 4
    own = lax.axis_index("expert") // (2 * SIDE)
    usable = (ids < 2) & (places < CAP)
    position = jnp.where(usable, ids * CAP + places, -1)
    next_position = back_one(position + 1) - 1
    next_g = back_one(g)

    oy, cy, oz, cz = pick(own.reshape(1), position, weights, x, g, split)

    zo = spread(oz)
    py = move(oy, PAIRED)
    mz = move(cz, MIRRORED)
    my = move(cy, MIRRORED)
    zc = spread(mz)
    qy = move(my, PAIRED)
    held = {}
    for name, here in ((OWN, oy), (PAIR, py), (MIRROR, my), (PAIRMIRROR, qy)):
        for where, piece in spread(here).items():
            held[where, name, 0] = piece
    for name, pair, ringed in ((OWN, PAIR, zo), (MIRROR, PAIRMIRROR, zc)):
        for where, piece in ringed.items():
            held[where, name, split] = piece
            held[where, pair, split] = jax.tree.map(lambda a: move(a, PAIRED), piece)
    pieces, table = [], []
    for (where, name, lo), piece in held.items():
        row = (where * 4 + name) * CAP
        hi = split if lo == 0 else width
        for kind, part in zip(("xs",) if where != FAR else ("x", "s"), jax.tree.leaves(piece)):
            pieces.append(part)
            table.append((row, lo, hi, kind))

    rows, grads, dgu, hidden, score = forward(pieces, tuple(table), wg, wu, wd, split)

    by = give_back(dgu, wg, wu, 0, split, 1024, "back_y")
    bz = give_back(dgu, wg, wu, split, width, 1024, "back_z")
    far_p = move(by[2 * FAR + 1], RIGHTWARD)
    far_o = move(by[2 * FAR], LEFTWARD)
    right_o = move(by[2 * RIGHT], RIGHTWARD)
    left_p = move(by[2 * LEFT + 1], LEFTWARD)
    right_p = move(add(by[2 * RIGHT + 1], far_p), RIGHTWARD)
    left_o = move(add(by[2 * LEFT], far_o), LEFTWARD)
    to_pair = move(add(by[2 * HERE + 1], right_p, left_p), PAIRED)
    sum_y = add(by[2 * HERE], right_o, left_o, to_pair)

    swapped = [move(bz[2 * where + 1], PAIRED) for where in range(4)]
    vz = [add(bz[2 * where], swapped[where]) for where in range(4)]
    far_oz = move(vz[FAR][:CAP], RIGHTWARD)
    far_cz = move(vz[FAR][CAP:], LEFTWARD)
    right_cz = move(vz[RIGHT][CAP:], RIGHTWARD)
    left_oz = move(vz[LEFT][:CAP], LEFTWARD)
    right_oz = move(add(vz[RIGHT][:CAP], far_oz), RIGHTWARD)
    left_cz = move(add(vz[LEFT][CAP:], far_cz), LEFTWARD)
    own_z = add(vz[HERE][:CAP], right_oz, left_oz)
    mirror_z = add(vz[HERE][CAP:], right_cz, left_cz)

    final_z = jnp.concatenate([back_one(own_z), back_one_mirrored(mirror_z)], axis=0)
    final_y = jnp.concatenate([back_one(sum_y[:CAP]), back_one_mirrored(sum_y[CAP:])], axis=0)
    hot = sum(m.astype(BF) for m in matches(next_position, own, tokens))
    joined = jnp.concatenate([final_y, final_z], axis=1)
    grown = jnp.dot(hot, joined, preferred_element_type=F32)
    previous = (next_g.astype(F32) + grown).astype(BF)

    first = (((0,), (0,)), ((), ()))
    down_grad = lax.dot_general(hidden, grads, first, preferred_element_type=F32).astype(BF)
    gate_grad = lax.dot_general(rows, dgu[:, :128], first, preferred_element_type=F32).astype(BF)
    up_grad = lax.dot_general(rows, dgu[:, 128:], first, preferred_element_type=F32).astype(BF)

    marks = score[:, 0].reshape(4, 4, CAP)
    here = marks[HERE]
    here = here + move(marks[RIGHT], RIGHTWARD)
    here = here + move(marks[LEFT], LEFTWARD)
    here = here + move(marks[FAR], ACROSS)
    mine = here[:2] + move(here[2:], PAIRED)
    other = move(mine[1], MIRRORED)
    total = jnp.concatenate([mine[0], other])[None, None, :]
    hit = jnp.stack(matches(position, own, tokens), axis=1)
    scored = jnp.sum(jnp.where(hit, total, 0.0), axis=2)
    router = jnp.where(usable, scored / weights.astype(F32), 0.0)
    return previous[None], gate_grad[None], up_grad[None], down_grad[None], router[None]


def solution(mesh):
    rows, cols = P("pipe", "expert", None), P("pipe", None, "expert")
    return jax.shard_map(
        shards,
        mesh=mesh,
        in_specs=(rows, rows, cols, cols, rows, rows, rows, rows),
        out_specs=(rows, cols, cols, rows, rows),
        check_vma=False,
    )
```

```python
import functools

import jax
import jax.numpy as jnp
from jax import lax
from jax.experimental import pallas as pl
from jax.experimental.pallas import tpu as pltpu
from jax.sharding import PartitionSpec as P


CAP = 32
SIDE = 4
LANES = 128
BF = jnp.bfloat16
F32 = jnp.float32


def ring(step):
    return [(z * SIDE + y, z * SIDE + (y + step) % SIDE) for z in range(SIDE) for y in range(SIDE)]


RIGHTWARD, LEFTWARD = ring(1), ring(-1)
PAIRED = [(e, e ^ SIDE) for e in range(SIDE * SIDE)]
MIRRORED = [(z * SIDE + y, (SIDE - 1 - z) * SIDE + y) for z in range(SIDE) for y in range(SIDE)]


def move(x, pairs):
    return lax.ppermute(x, "expert", pairs)


def back_one(x):
    size = lax.axis_size("pipe")
    return lax.ppermute(x, "pipe", [(i, i - 1) for i in range(1, size)])


def back_one_mirrored(x):
    size = lax.axis_size("pipe")
    pairs = [(e * size + i, m * size + i - 1) for e, m in MIRRORED for i in range(1, size)]
    return lax.ppermute(x, ("expert", "pipe"), pairs)


def wanted(own, tokens):
    row = lax.broadcasted_iota(jnp.int32, (2 * CAP, tokens), 0)
    expert = jnp.where(row < CAP, own, 1 - own)
    return expert * CAP + row % CAP + 1


def whole(a):
    return pl.BlockSpec(a.shape, lambda *_: (0,) * len(a.shape))


def pick_kernel(own_ref, ids_ref, slots_ref, w_ref, x_ref, g_ref, o, cx, cs, pos_ref, hot, scale):
    @pl.when(pl.program_id(0) == 0)
    def _():
        ids, slots = ids_ref[...], slots_ref[...]
        position = jnp.where((ids < 2) & (slots < CAP), ids * CAP + slots + 1, 0)
        pos_ref[...] = position
        weights = w_ref[...].astype(F32)
        target = wanted(own_ref[0], ids.shape[1])
        weight = jnp.zeros(target.shape, F32)
        for k in range(ids.shape[0]):
            hit = position[k : k + 1, :] == target
            weight = weight + jnp.where(hit, weights[k : k + 1, :], 0.0)
        hot[...] = jnp.where(weight > 0.0, 1.0, 0.0).astype(BF)
        scale[...] = jnp.broadcast_to(jnp.sum(weight, axis=1, keepdims=True), scale.shape)

    x = jnp.dot(hot[...], x_ref[...], preferred_element_type=F32).astype(BF)
    g = jnp.dot(hot[...], g_ref[...], preferred_element_type=F32)
    s = (g * scale[:, 0:1]).astype(BF)
    o[0:CAP, :] = x[0:CAP]
    o[CAP : 2 * CAP, :] = s[0:CAP]
    cx[...] = x[CAP : 2 * CAP]
    cs[...] = s[CAP : 2 * CAP]


def pick(own, ids, slots, weights, x, g, block=1024):
    tokens, width = x.shape
    cols = lambda n: pl.BlockSpec((n, block), lambda j, *_: (0, j))
    shape = lambda n: jax.ShapeDtypeStruct((n, width), BF)
    return pl.pallas_call(
        pick_kernel,
        grid_spec=pltpu.PrefetchScalarGridSpec(
            num_scalar_prefetch=1,
            grid=(width // block,),
            in_specs=[whole(ids), whole(slots), whole(weights), cols(tokens), cols(tokens)],
            out_specs=[cols(2 * CAP), cols(CAP), cols(CAP), whole(ids)],
            scratch_shapes=[pltpu.VMEM((2 * CAP, tokens), BF), pltpu.VMEM((2 * CAP, LANES), F32)],
        ),
        out_shape=[shape(2 * CAP), shape(CAP), shape(CAP), jax.ShapeDtypeStruct(ids.shape, jnp.int32)],
        name="pick",
    )(own, ids, slots, weights, x, g)


def member_kernel(*refs, places, kept, base, n_in, chunk):
    n = len(places)
    pieces, (wg, wu, wd) = refs[:n], refs[n : n + 3]
    xo, so, dgu, hid = refs[n_in : n_in + 4]
    backs = refs[n_in + 4 : n_in + 4 + len(kept)]
    x, s, wgu, wdv, agu, ab, out, sems, osem = refs[n_in + 4 + len(kept) :]
    rows, width = x.shape
    half = width // 2
    stages = []
    k = 0
    for lo in (0, half):
        at = pl.ds(lo, half)
        moves = [
            (wg.at[at], wgu.at[at, 0:LANES]),
            (wu.at[at], wgu.at[at, LANES : 2 * LANES]),
            (wd.at[:, at], wdv.at[:, at]),
        ]
        for ref, (row, kind) in zip(pieces, places):
            for i, letter in enumerate(kind):
                dst = x if letter == "x" else s
                moves.append((ref.at[i * CAP : (i + 1) * CAP, at], dst.at[row : row + CAP, at]))
        stages.append([])
        for src, dst in moves:
            stages[-1].append(pltpu.make_async_copy(src, dst, sems.at[k]))
            k += 1
    for copy in stages[0] + stages[1]:
        copy.start()
    agu[...] = jnp.zeros_like(agu)
    ab[...] = jnp.zeros_like(ab)
    across = (((1,), (1,)), ((), ()))
    sent = []
    k = 0

    def send(src, dst):
        nonlocal k
        copy = pltpu.make_async_copy(src, dst, osem.at[k])
        copy.start()
        sent.append(copy)
        k += 1

    for i, lo in enumerate((0, half)):
        for copy in stages[i]:
            copy.wait()
        for src, dst in ((x, xo), (s, so)):
            send(src.at[:, pl.ds(lo, half)], dst.at[pl.ds(base, rows), pl.ds(lo, half)])

        def gather(j, _, lo=lo):
            at = pl.ds(pl.multiple_of(lo + j * chunk, LANES), chunk)
            agu[...] += jnp.dot(x[:, at], wgu[at, :], preferred_element_type=F32)
            ab[...] += lax.dot_general(s[:, at], wdv[:, at], across, preferred_element_type=F32)
            return 0

        lax.fori_loop(0, half // chunk, gather, 0)
    gate, up, back = agu[:, 0:LANES], agu[:, LANES : 2 * LANES], ab[...]
    sigmoid = jax.nn.sigmoid(gate)
    silu = gate * sigmoid
    hidden = (silu * up).astype(BF)
    hid[...] = hidden
    dgu[:, 0:LANES] = (back * up * sigmoid * (1.0 + gate * (1.0 - sigmoid))).astype(BF)
    dgu[:, LANES : 2 * LANES] = (back * silu).astype(BF)
    total = jnp.sum(hidden.astype(F32) * back, axis=1, keepdims=True)
    out[:, width : width + LANES] = jnp.broadcast_to(total, (rows, LANES)).astype(BF)

    for lo, hi in ((0, half), (half, width)):

        def scatter(j, _, lo=lo):
            at = pl.ds(pl.multiple_of(lo + j * chunk, LANES), chunk)
            value = lax.dot_general(dgu[...], wgu[at, :], across, preferred_element_type=F32)
            out[:, at] = value.astype(BF)
            return 0

        lax.fori_loop(0, half // chunk, scatter, 0)
        end = hi if lo == 0 else width + LANES
        for row, dst in zip(kept, backs):
            send(out.at[row : row + CAP, lo:end], dst.at[:, lo:end])
    for copy in sent:
        copy.wait()


def member(pieces, places, kept, wg, wu, wd, base, total, carried=None, chunk=896, name="member"):
    width, units = wg.shape
    rows = sum(len(kind) for _, kind in places) // 2 * CAP
    copies = 2 * (3 + sum(len(kind) for _, kind in places))
    anywhere = pl.BlockSpec(memory_space=pl.ANY)
    vmem = pl.BlockSpec(memory_space=pltpu.VMEM)
    operands = [*pieces, wg, wu, wd] + ([] if carried is None else list(carried))
    n_in = len(operands)
    return pl.pallas_call(
        functools.partial(
            member_kernel, places=places, kept=kept, base=base, n_in=n_in, chunk=chunk
        ),
        in_specs=[anywhere] * n_in,
        out_specs=[anywhere, anywhere, vmem, vmem] + [anywhere] * len(kept),
        out_shape=[
            jax.ShapeDtypeStruct((total, width), BF),
            jax.ShapeDtypeStruct((total, width), BF),
            jax.ShapeDtypeStruct((rows, 2 * units), BF),
            jax.ShapeDtypeStruct((rows, units), BF),
        ]
        + [jax.ShapeDtypeStruct((CAP, width + LANES), BF)] * len(kept),
        scratch_shapes=[
            pltpu.VMEM((rows, width), BF),
            pltpu.VMEM((rows, width), BF),
            pltpu.VMEM((width, 2 * units), BF),
            pltpu.VMEM((units, width), BF),
            pltpu.VMEM((rows, 2 * units), F32),
            pltpu.VMEM((rows, units), F32),
            pltpu.VMEM((rows, width + LANES), BF),
            pltpu.SemaphoreType.DMA((copies,)),
            pltpu.SemaphoreType.DMA((4 + 2 * len(kept),)),
        ],
        input_output_aliases={} if carried is None else {n_in - 2: 0, n_in - 1: 1},
        name=name,
    )(*operands)


def combine_kernel(own_ref, pos_ref, g_ref, o_ref, c_ref, out_ref, hot):
    @pl.when(pl.program_id(0) == 0)
    def _():
        position = pos_ref[...]
        target = wanted(own_ref[0], position.shape[1])
        one = jnp.zeros(target.shape, F32)
        for k in range(position.shape[0]):
            one = one + jnp.where(position[k : k + 1, :] == target, 1.0, 0.0)
        hot[...] = one.astype(BF)

    dims = (((0,), (0,)), ((), ()))
    grown = lax.dot_general(hot[0:CAP, :], o_ref[...], dims, preferred_element_type=F32)
    grown += lax.dot_general(hot[CAP : 2 * CAP, :], c_ref[...], dims, preferred_element_type=F32)
    out_ref[...] = (g_ref[...].astype(F32) + grown).astype(BF)


def combine(own, position, g, o, c, block=1024):
    tokens, width = g.shape
    cols = lambda n: pl.BlockSpec((n, block), lambda j, *_: (0, j))
    return pl.pallas_call(
        combine_kernel,
        grid_spec=pltpu.PrefetchScalarGridSpec(
            num_scalar_prefetch=1,
            grid=(width // block,),
            in_specs=[whole(position), cols(tokens), cols(CAP), cols(CAP)],
            out_specs=cols(tokens),
            scratch_shapes=[pltpu.VMEM((2 * CAP, tokens), BF)],
        ),
        out_shape=jax.ShapeDtypeStruct(g.shape, BF),
        name="combine",
    )(own, position, g, o, c)


def router_kernel(own_ref, pos_ref, w_ref, o_ref, c_ref, out_ref):
    position = pos_ref[...]
    target = wanted(own_ref[0], position.shape[1])
    score = jnp.concatenate([o_ref[:, 0:1], c_ref[:, 0:1]], axis=0).astype(F32)
    weights = w_ref[...].astype(F32)
    for k in range(position.shape[0]):
        hit = jnp.where(position[k : k + 1, :] == target, score, 0.0)
        out_ref[k : k + 1, :] = jnp.sum(hit, axis=0, keepdims=True) / weights[k : k + 1, :]


def router(own, position, weights, o, c):
    vmem = pl.BlockSpec(memory_space=pltpu.VMEM)
    return pl.pallas_call(
        router_kernel,
        in_specs=[pl.BlockSpec(memory_space=pltpu.SMEM)] + [vmem] * 4,
        out_specs=vmem,
        out_shape=jax.ShapeDtypeStruct(position.shape, F32),
        name="router",
    )(own, position, weights, o, c)


def add(*terms):
    total = terms[0].astype(F32)
    for term in terms[1:]:
        total = total + term.astype(F32)
    return total.astype(BF)


def along_y(x, s):
    left = (move(x, RIGHTWARD), move(s, RIGHTWARD))
    right = (move(x, LEFTWARD), move(s, LEFTWARD))
    return left, right, (move(left[0], RIGHTWARD), move(right[1], LEFTWARD))


def shards(x, g, wg, wu, wd, expert_ids, slots, weights):
    x, g, wg, wu, wd = x[0], g[0], wg[0], wu[0], wd[0]
    ids, slots, weights = expert_ids[0].T, slots[0].T, weights[0].T
    width = x.shape[1]
    own = (lax.axis_index("expert") // (2 * SIDE)).reshape(1)

    o, cx, cs, position = pick(own, ids, slots, weights, x, g)
    o_left, o_right = move(o, RIGHTWARD), move(o, LEFTWARD)
    p = move(o, PAIRED)
    cx, cs = move(cx, MIRRORED), move(cs, MIRRORED)
    qx, qs = move(cx, PAIRED), move(cs, PAIRED)
    c_left, c_right, c_far = along_y(cx, cs)
    o_far = (move(o_left[:CAP], RIGHTWARD), move(o_right[CAP:], LEFTWARD))
    p_left, p_right = move(o_left, PAIRED), move(o_right, PAIRED)
    p_far = (move(o_far[0], PAIRED), move(o_far[1], PAIRED))
    q_left, q_right, q_far = along_y(qx, qs)
    next_g = back_one(g)
    next_position = back_one(position)

    first = {
        "oh": o, "ol": o_left, "or": o_right, "of": o_far, "ph": p, "pl": p_left, "pr": p_right,
        "ch": (cx, cs), "cl": c_left, "cr": c_right, "cf": c_far,
        "qh": (qx, qs), "ql": q_left, "qr": q_right,
    }
    second = {"pf": p_far, "qf": q_far}

    def run(blocks, base, carried=None, name="member"):
        pieces, places = [], []
        for i, piece in enumerate(blocks.values()):
            parts = piece if isinstance(piece, tuple) else (piece,)
            for part, kind in zip(parts, ("x", "s") if len(parts) == 2 else ("xs",)):
                pieces.append(part)
                places.append((i * CAP, kind))
        kept = tuple(i * CAP for i in range(len(blocks)))
        xo, so, dgu, hid, *backs = member(
            pieces, tuple(places), kept, wg, wu, wd, base, 16 * CAP, carried, name=name
        )
        return xo, so, dgu, hid, dict(zip(blocks, backs))

    rows, grads, dgu1, hid1, b = run(first, 0, name="member_first")
    rows, grads, dgu2, hid2, b2 = run(
        second, len(first) * CAP, (rows, grads), name="member_second"
    )
    b.update(b2)

    right_q, left_c = move(b["qr"], RIGHTWARD), move(b["cl"], LEFTWARD)
    far_c, far_q = move(b["cf"], RIGHTWARD), move(b["qf"], LEFTWARD)
    p_right, p_left = move(b["pr"], PAIRED), move(b["pl"], PAIRED)
    p_far, p_here = move(b["pf"], PAIRED), move(b["ph"], PAIRED)
    right_c = move(add(b["cr"], far_c), RIGHTWARD)
    left_q = move(add(b["ql"], far_q), LEFTWARD)
    q_here = move(add(b["qh"], right_q, left_q), PAIRED)
    cut = CAP // 2
    far_o = add(b["of"], p_far)
    far_a, far_b = move(far_o[:cut], RIGHTWARD), move(far_o[cut:], LEFTWARD)
    right_o = jnp.concatenate(
        [add(b["or"][:cut], p_right[:cut], far_a), add(b["or"][cut:], p_right[cut:])]
    )
    left_o = jnp.concatenate(
        [add(b["ol"][:cut], p_left[:cut]), add(b["ol"][cut:], p_left[cut:], far_b)]
    )
    right_o, left_o = move(right_o, RIGHTWARD), move(left_o, LEFTWARD)
    mirror = add(b["ch"], right_c, left_c, q_here)
    home = add(b["oh"], p_here, right_o, left_o)

    final_c, final_o = back_one_mirrored(mirror), back_one(home)
    mirror_score = move(mirror[:, width:], MIRRORED)
    previous = combine(own, next_position, next_g, final_o, final_c)
    scored = router(own, position, weights, home[:, width:], mirror_score)

    dgu = jnp.concatenate([dgu1, dgu2])
    hid = jnp.concatenate([hid1, hid2])
    contract = (((0,), (0,)), ((), ()))
    grads, hid, _ = lax.optimization_barrier((grads, hid, far_c))
    down_grad = lax.dot_general(hid, grads, contract, preferred_element_type=F32).astype(BF)
    rows, dgu, _ = lax.optimization_barrier((rows, dgu, far_q))
    gate_grad = lax.dot_general(rows, dgu[:, :LANES], contract, preferred_element_type=F32)
    up_grad = lax.dot_general(rows, dgu[:, LANES:], contract, preferred_element_type=F32)
    return (
        previous[None],
        gate_grad.astype(BF)[None],
        up_grad.astype(BF)[None],
        down_grad[None],
        scored.T[None],
    )


def solution(mesh):
    rows, cols = P("pipe", "expert", None), P("pipe", None, "expert")
    return jax.shard_map(
        shards,
        mesh=mesh,
        in_specs=(rows, rows, cols, cols, rows, rows, rows, rows),
        out_specs=(rows, cols, cols, rows, rows),
        check_vma=False,
    )
```
